32 devices in a mesh: parts: 2 (over x), owner: 16 (over z, y, core).
Axes of the slice: x: 2, y: 2, z: 4, core: 2. Of those that a mesh axis runs over, the one named last changes fastest.
Arguments:
- embeddings: bfloat16 [32768, 512], P(('parts', 'owner')), parts along dimension 0, may hold values from -6 to 6
- cluster: int32 [32768], P(('parts', 'owner')), parts along dimension 0, may hold values from 0 to 7
- lengths: int32 [32, 16], P(('parts', 'owner')), parts along dimension 0, may hold values from 1 to 64, 896 in all within a row
Outputs:
- best: float32 [32768], P(('parts', 'owner')), parts along dimension 0
The draws below stay inside these ranges and needn't reach their ends.
There are 2 independent parts, one for each index of `parts`. The reference program is written for one: setup_inputs(seed, part) draws one part's arguments, and reference() takes and returns one part's arrays. A program takes and returns all parts, laid end to end along the dimension named above; each array names one. Nothing has to cross between parts.
Inputs may be any that keep to these rules, and one draw needn't show every extreme that they name: Each row of lengths sums to 896 and reaches 64 in some column.
All inputs are finite; a program needn't handle non-finite values.
Results may differ from the reference program's by a relative error of at most 0.00049.
Values may be sent and summed in bfloat16 or wider, within the bound.
No kernel may reach another device: no remote copies, remote signals or barrier semaphores. Data moves between devices by JAX's collectives and lax.ppermute only.
A program may use at most 64 MiB of HBM per device.

```python
import math
import jax
import jax.numpy as jnp
import numpy as np
from jax import lax

E = 512
CAP = 64
C_DEV = 8
ROWS = 16384
N_OWNER = 16


def touch_ends(drawn, rng, smallest, high):
    longest = drawn.shape.index(max(drawn.shape))
    spots = []
    for shift in (0, 1):
        where = [jax.random.randint(jax.random.fold_in(rng, axis), (), 0, length) for axis, length in enumerate(drawn.shape)]
        where[longest] = (where[longest] + shift) % drawn.shape[longest]
        spots.append(tuple(where))
    return drawn.at[spots[0]].set(smallest).at[spots[1]].set(high)


def steps_of(own_key, shape, shards, low, top_value):
    def one(axis_at, parts):
        heights = jax.random.uniform(jax.random.fold_in(jax.random.fold_in(own_key, 6), axis_at), (parts,), jnp.float32, low / len(shards), top_value / len(shards))
        return jnp.repeat(jnp.exp(heights), shape[axis_at] // parts).reshape((-1,) + (1,) * (len(shape) - axis_at - 1))

    level = one(*shards[0])
    for cut in shards[1:]:
        level = level * one(*cut)
    return level


def rank_table(count, skew):
    loads = [(1 << 20) // math.isqrt(standing ** skew) + 1 for standing in range(1, count + 1)]
    spread = 1 + sum(loads) // (1 << 30)
    return np.cumsum(np.array([max(1, weight // spread) for weight in loads]))


def skewed_ids(stream_key, shape, amount, lean):
    grid = rank_table(amount, lean)
    ticket = jax.random.randint(jax.random.fold_in(stream_key, 1), shape, 0, int(grid[amount - 1]))
    rank = jnp.searchsorted(jnp.asarray(grid, jnp.int32), ticket, side="right")
    return jax.random.permutation(jax.random.fold_in(stream_key, 2), amount)[rank].astype(jnp.int32)


def profile(count, total, reach, slope):
    portions = [(1 << 20) // math.isqrt(standing ** slope) + 1 for standing in range(2, count + 1)]
    rest, given = total - reach - (count - 1), [1] * (count - 1)
    while rest > 0:
        candidates = [i for i in range(count - 1) if given[i] < reach]
        mass, remaining = sum([portions[i] for i in candidates]), rest
        for i in candidates:
            extra = min(reach - given[i], max(1, remaining * portions[i] // mass), rest)
            given[i] = given[i] + extra
            rest = rest - extra
    return np.array([reach] + given)


def uneven_parts(stream_key, number_of, total, most, skew):
    if number_of == 2:
        one = jax.random.randint(stream_key, (), max(1, total - most), min(most, total - 1) + 1)
        return jnp.stack([one, total - one])
    sizes = jnp.asarray(profile(number_of, total, most, skew), jnp.int32)
    couples = (number_of - 1) // 2
    source_of, sink = sizes[1:1 + 2 * couples:2], sizes[2:2 + 2 * couples:2]
    room = jnp.minimum(source_of - 1, most - sink)
    shifted = jax.random.randint(jax.random.fold_in(stream_key, 1), (couples,), 0, 1 << 20) % (room + 1)
    sizes = sizes.at[1:1 + 2 * couples:2].set(source_of - shifted).at[2:2 + 2 * couples:2].set(sink + shifted)
    return sizes[jax.random.permutation(jax.random.fold_in(stream_key, 2), number_of)]


def centred(rng, dims, scale, bound, shards=(), kind=jnp.bfloat16):
    result = jax.random.normal(rng, dims, jnp.float32) * scale
    if len(shards) > 0:
        result = steps_of(rng, dims, shards, -0.22, 0.18) * result
    return jnp.clip(result, min=-bound, max=bound).astype(kind)


def setup_inputs(seed: int = 0, part: int = 0) -> dict:
    keys = jax.random.split(jax.random.key(seed), 4)
    own_keys = jax.random.split(jax.random.fold_in(keys[3], part), 4)
    embeddings = centred(own_keys[0], (ROWS, E), 1.0, 6.0, ((0, 16),))
    cluster = touch_ends(skewed_ids(own_keys[1], (ROWS,), C_DEV, 2), jax.random.fold_in(own_keys[1], 3), 0, C_DEV - 1).astype(jnp.int32)
    lengths = jax.vmap(lambda own: uneven_parts(own, N_OWNER, N_OWNER * CAP - N_OWNER * CAP // 8, CAP, 2))(jax.random.split(own_keys[2], N_OWNER)).reshape((N_OWNER, N_OWNER)).astype(jnp.int32)
    return {"embeddings": embeddings, "cluster": cluster, "lengths": lengths}


def normalize(embeddings):
    values = embeddings.astype(jnp.float32)
    factor = lax.rsqrt(lax.optimization_barrier(jnp.mean(values * values, axis=-1, keepdims=True)) + 1e-06) / math.sqrt(E)
    return (values * factor).astype(jnp.bfloat16)

def owner_best(pair):
    units, labels = pair
    similar = jnp.dot(units, units.T, preferred_element_type=jnp.float32)
    count = units.shape[0]
    index = jnp.arange(count, dtype=jnp.int32)
    same_group = (labels[:, None] == labels[None, :]) & (labels[:, None] >= 0) & (index[:, None] != index[None, :])
    return lax.optimization_barrier(jnp.max(jnp.where(same_group, similar, jnp.float32(-1.0)), axis=1))

def reference(embeddings, cluster, lengths):
    owners = N_OWNER
    units = normalize(embeddings)
    total = owners * owners * CAP
    slots = jnp.arange(total, dtype=jnp.int32)
    limits = jnp.repeat(lengths.reshape(-1), CAP, total_repeat_length=total)
    live = slots % CAP < limits
    labels = jnp.where(live, cluster, -1).astype(jnp.int32)
    grouped = units.reshape(owners, owners, CAP, E).transpose(1, 0, 2, 3).reshape(owners, owners * CAP, E)
    grouped_labels = labels.reshape(owners, owners, CAP).transpose(1, 0, 2).reshape(owners, owners * CAP)
    results = lax.map(owner_best, (grouped, grouped_labels))
    return results.reshape(owners, owners, CAP).transpose(1, 0, 2).reshape(total)
```

```python
import functools
import math

import jax
import jax.numpy as jnp
from jax import lax
from jax.experimental import pallas as pl
from jax.experimental.pallas import tpu as pltpu
from jax.sharding import PartitionSpec as P


LANES = 128
EXTRA = 8


def normalize(block, width):
    values = block.astype(jnp.float32)
    mean = jnp.mean(values * values, axis=-1, keepdims=True)
    factor = lax.rsqrt(mean + 1e-06) / math.sqrt(width)
    return (values * factor).astype(jnp.bfloat16)


def label_row(block, capacity, lengths_ref, cluster_ref):
    per_row = LANES // capacity
    row = cluster_ref[pl.ds(block // per_row, 1), :]
    lane = lax.broadcasted_iota(jnp.int32, (1, LANES), 1)
    part = block % per_row
    kept = jnp.where(lane // capacity == part, row, 0)
    spread = kept
    for step in range(1, per_row):
        spread = spread + pltpu.roll(kept, step * capacity, 1)
    return jnp.where(lane % capacity < lengths_ref[0, block], spread, -1)


def pack_kernel(keys, capacity, width, me_ref, lengths_ref, cluster_ref, *refs):
    chunks = width // LANES
    count = len(keys)
    for key, source, target in zip(keys, refs[:count], refs[count:]):
        block = jnp.bitwise_xor(me_ref[0], key)
        units = normalize(source[...], width)
        for chunk in range(chunks):
            target[pl.ds(chunk * capacity, capacity), :] = units[:, chunk * LANES:(chunk + 1) * LANES]
        labels = label_row(block, capacity, lengths_ref, cluster_ref).astype(jnp.float32)
        target[pl.ds(chunks * capacity, EXTRA), :] = jnp.broadcast_to(labels, (EXTRA, LANES)).astype(jnp.bfloat16)


def pack(keys, me, lengths, cluster, embeddings, capacity):
    width = embeddings.shape[1]
    packed_rows = capacity * (width // LANES) + EXTRA

    def block_spec(key):
        return pl.BlockSpec((capacity, width), lambda i, me_ref, lengths_ref: (jnp.bitwise_xor(me_ref[0], key), 0))

    return pl.pallas_call(
        functools.partial(pack_kernel, keys, capacity, width),
        out_shape=[jax.ShapeDtypeStruct((packed_rows, LANES), jnp.bfloat16)] * len(keys),
        grid_spec=pltpu.PrefetchScalarGridSpec(
            num_scalar_prefetch=2,
            grid=(1,),
            in_specs=[pl.BlockSpec(cluster.shape, lambda i, *_: (0, 0))] + [block_spec(key) for key in keys],
            out_specs=[pl.BlockSpec((packed_rows, LANES), lambda i, *_: (0, 0)) for _ in keys],
        ),
        name="pack",
    )(me, lengths, cluster, *[embeddings] * len(keys))


def best_kernel(capacity, width, me_ref, *refs):
    blocks = len(refs) - 3
    sources, target, units, = refs[:blocks], refs[blocks], refs[blocks + 1]
    chunks = width // LANES
    per_row = LANES // capacity
    lane = lax.broadcasted_iota(jnp.int32, (1, LANES), 1)
    label_rows = []
    for key, source in enumerate(sources):
        for chunk in range(chunks):
            units[pl.ds(key * capacity, capacity), pl.ds(chunk * LANES, LANES)] = source[pl.ds(chunk * capacity, capacity), :]
        label_rows.append(source[pl.ds(chunks * capacity, EXTRA), :].astype(jnp.float32))
    merged = []
    for first in range(0, blocks, per_row):
        row = label_rows[first]
        for part in range(1, per_row):
            row = jnp.where(lane // capacity == part, label_rows[first + part], row)
        merged.append(row)
    labels = jnp.concatenate(merged, axis=1)
    rows = blocks * capacity
    columns = jnp.transpose(labels)[:, :1]
    labels_here = labels[:1]
    labels_here = jnp.where(labels_here < 0, -2.0, labels_here)
    tile = min(256, rows)
    running = jnp.full((8, rows), -1.0, jnp.float32)
    for start in range(0, rows, tile):
        similar = lax.dot_general(
            units[pl.ds(start, tile), :], units[...], (((1,), (1,)), ((), ())), preferred_element_type=jnp.float32
        )
        same = columns[start:start + tile] == labels_here
        masked = jnp.where(same, similar, -1.0)
        own = masked[:, start:start + tile]
        off = lax.broadcasted_iota(jnp.int32, (tile, tile), 0) != lax.broadcasted_iota(jnp.int32, (tile, tile), 1)
        own = jnp.where(off, own, -1.0)
        pieces = [masked[:, :start]] if start else []
        pieces.append(own)
        if start + tile < rows:
            pieces.append(masked[:, start + tile:])
        masked = jnp.concatenate(pieces, axis=1) if len(pieces) > 1 else pieces[0]
        running = jnp.maximum(running, jnp.max(masked.reshape(tile // 8, 8, rows), axis=0))
    best = jnp.max(running, axis=0, keepdims=True)
    for key in range(blocks):
        first = key * capacity // LANES * LANES
        piece = best[:, first:first + LANES]
        kept = jnp.where(lane // capacity == key % per_row, piece, 0.0)
        spread = kept
        for step in range(1, per_row):
            spread = spread + pltpu.roll(kept, step * capacity, 1)
        target[jnp.bitwise_xor(me_ref[0], key)] = spread


def owner_best(me, packed, capacity, width):
    blocks = len(packed)
    rows = blocks * capacity
    return pl.pallas_call(
        functools.partial(best_kernel, capacity, width),
        out_shape=jax.ShapeDtypeStruct((blocks, 1, LANES), jnp.float32),
        in_specs=[pl.BlockSpec(memory_space=pltpu.SMEM)] + [pl.BlockSpec(memory_space=pltpu.VMEM)] * blocks,
        out_specs=pl.BlockSpec(memory_space=pltpu.VMEM),
        scratch_shapes=[pltpu.VMEM((rows, width), jnp.bfloat16), pltpu.VMEM((8, LANES), jnp.float32)],
        compiler_params=pltpu.CompilerParams(vmem_limit_bytes=rows * (width * 4 + 4096) + (8 << 20)),
        name="best",
    )(me, *packed)


def finish_kernel(capacity, source, target):
    per_row = LANES // capacity
    lane = lax.broadcasted_iota(jnp.int32, (1, LANES), 1)
    for row in range(target.shape[0]):
        value = source[row * per_row]
        for part in range(1, per_row):
            value = jnp.where(lane // capacity == part, source[row * per_row + part], value)
        target[pl.ds(row, 1), :] = value


def finish(returned, capacity):
    rows = returned.shape[0] * capacity // LANES
    return pl.pallas_call(
        functools.partial(finish_kernel, capacity),
        out_shape=jax.ShapeDtypeStruct((rows, LANES), jnp.float32),
        in_specs=[pl.BlockSpec(memory_space=pltpu.VMEM)],
        out_specs=pl.BlockSpec(memory_space=pltpu.VMEM),
        name="finish",
    )(returned)


def send_order(owners):
    half, quarter = owners // 2, owners // 4
    return list(range(half + quarter, owners)) + list(range(half, half + quarter)) + list(range(half - 1, 0, -1))


def on_device(embeddings, cluster, lengths):
    owners = lax.axis_size("owner")
    rows_here, width = embeddings.shape
    capacity = rows_here // owners
    me = lax.axis_index("owner").astype(jnp.int32).reshape(1)
    cluster = cluster.reshape(rows_here // LANES, LANES)
    order = send_order(owners)
    early = tuple(order[:2])
    late = tuple(order[2:]) + (0,)
    packed = dict(zip(early, pack(early, me, lengths, cluster, embeddings, capacity)))
    packed.update(zip(late, pack(late, me, lengths, cluster, embeddings, capacity)))
    got = {0: packed[0]}
    for key in order:
        got[key] = lax.ppermute(packed[key], "owner", [(i, i ^ key) for i in range(owners)])
    found = owner_best(me, [got[key] for key in range(owners)], capacity, width)
    returned = lax.all_to_all(found, "owner", split_axis=0, concat_axis=0, tiled=True)
    return finish(returned, capacity).reshape(rows_here)


def solution(mesh):
    return jax.shard_map(
        on_device,
        mesh=mesh,
        in_specs=(P(("parts", "owner"), None), P(("parts", "owner")), P(("parts", "owner"), None)),
        out_specs=P(("parts", "owner")),
        check_vma=False,
    )
```

```python
import functools
import math

import jax
import jax.numpy as jnp
from jax import lax
from jax.experimental import pallas as pl
from jax.experimental.pallas import tpu as pltpu
from jax.sharding import PartitionSpec as P


LANES = 128
EXTRA = 8
TILE = 1 << 20
ORDER = (6, 2, 5, 3, 1, 4, 7)
CUT = 1


def normalize(block, width):
    values = block.astype(jnp.float32)
    mean = jnp.mean(values * values, axis=-1, keepdims=True)
    factor = lax.rsqrt(mean + 1e-06) / math.sqrt(width)
    return (values * factor).astype(jnp.bfloat16)


def label_row(block, capacity, lengths_ref, cluster_ref):
    row = cluster_ref[pl.ds(block // 2, 1), :]
    lane = lax.broadcasted_iota(jnp.int32, (1, LANES), 1)
    kept = jnp.where(lane // capacity == block % 2, row, 0)
    spread = kept + pltpu.roll(kept, capacity, 1)
    owner = lax.broadcasted_iota(jnp.int32, lengths_ref.shape, 1)
    limit = jnp.sum(jnp.where(owner == block, lengths_ref[...], 0), axis=1, keepdims=True)
    return jnp.where(lane % capacity < limit, spread, -1)


def pack_kernel(items, capacity, width, embeddings, lengths, cluster, *refs):
    count = len(items)
    targets, (blocks, lengths_here, cluster_here, arrived) = refs[:count], refs[count:]
    chunks = width // LANES
    me = lax.axis_index("owner")
    keys = [key for item in items for key in item]
    copies = []
    for index, key in enumerate(keys):
        first = pl.multiple_of(jnp.bitwise_xor(me, key) * capacity, capacity)
        copies.append(pltpu.make_async_copy(embeddings.at[pl.ds(first, capacity), :], blocks.at[index], arrived.at[index]))
    small = [
        pltpu.make_async_copy(lengths, lengths_here, arrived.at[len(keys)]),
        pltpu.make_async_copy(cluster, cluster_here, arrived.at[len(keys) + 1]),
    ]
    for copy in copies[:1] + small + copies[1:]:
        copy.start()
    for copy in small + copies:
        copy.wait()
    lane = lax.broadcasted_iota(jnp.int32, (1, LANES), 1)
    for item, target in zip(items, targets):
        rows = [label_row(jnp.bitwise_xor(me, key), capacity, lengths_here, cluster_here) for key in item]
        labels = rows[0] if len(rows) == 1 else jnp.where(lane < capacity, rows[0], rows[1])
        labels = jnp.broadcast_to(labels.astype(jnp.float32), (EXTRA, LANES)).astype(jnp.bfloat16)
        target[pl.ds(len(item) * chunks * capacity, EXTRA), :] = labels
    index = 0
    for item, target in zip(items, targets):
        for part in range(len(item)):
            units = normalize(blocks[index], width)
            for chunk in range(chunks):
                first = (part * chunks + chunk) * capacity
                target[pl.ds(first, capacity), :] = units[:, chunk * LANES:(chunk + 1) * LANES]
            index += 1


def pack(items, lengths, cluster, embeddings, capacity):
    width = embeddings.shape[1]
    chunks = width // LANES
    keys = sum(len(item) for item in items)
    inputs = [pltpu.with_memory_space_constraint(a, pltpu.HBM) for a in (embeddings, lengths, cluster)]
    return pl.pallas_call(
        functools.partial(pack_kernel, items, capacity, width),
        out_shape=[
            jax.ShapeDtypeStruct((len(item) * chunks * capacity + EXTRA, LANES), jnp.bfloat16) for item in items
        ],
        in_specs=[pl.BlockSpec(memory_space=pltpu.HBM)] * 3,
        out_specs=vmem(len(items)),
        scratch_shapes=[
            pltpu.VMEM((keys, capacity, width), jnp.bfloat16),
            pltpu.VMEM(lengths.shape, jnp.int32),
            pltpu.VMEM(cluster.shape, jnp.int32),
            pltpu.SemaphoreType.DMA((keys + 2,)),
        ],
        compiler_params=pltpu.CompilerParams(vmem_limit_bytes=keys * capacity * width * 6 + (4 << 20)),
        name="pack",
    )(*inputs)


def unpack(sources, parts, units, capacity, chunks):
    lane = lax.broadcasted_iota(jnp.int32, (1, LANES), 1)
    rows = []
    for index, (source, part) in enumerate(zip(sources, parts)):
        for chunk in range(chunks):
            value = source[pl.ds((part * chunks + chunk) * capacity, capacity), :]
            units[pl.ds(index * capacity, capacity), pl.ds(chunk * LANES, LANES)] = value
        rows.append(source[pl.ds(source.shape[0] - EXTRA, EXTRA), :].astype(jnp.float32))
    merged = [jnp.where(lane < capacity, rows[index], rows[index + 1]) for index in range(0, len(rows), 2)]
    return jnp.concatenate(merged, axis=1) if len(merged) > 1 else merged[0]


def as_columns(labels):
    return jnp.transpose(labels)[:, :1]


def similarity(left, right):
    return lax.dot_general(left, right, (((1,), (1,)), ((), ())), preferred_element_type=jnp.float32)


def pieces_of(columns, row_labels, left, right, first):
    similar = similarity(left, right)
    alive = jnp.where(row_labels < 0, -2.0, row_labels)
    masked = jnp.where(columns == alive, similar, -1.0)
    tiles = [masked[:, start:start + LANES] for start in range(0, masked.shape[1], LANES)]
    if first is not None:
        row = lax.broadcasted_iota(jnp.int32, (left.shape[0], LANES), 0)
        lane = lax.broadcasted_iota(jnp.int32, (left.shape[0], LANES), 1)
        for start in range(0, left.shape[0], LANES):
            own = (first + start) // LANES
            tiles[own] = jnp.where(row != lane + start, tiles[own], -1.0)
    return tiles


def fold(tile):
    return jnp.max(tile.reshape(tile.shape[0] // EXTRA, EXTRA, LANES), axis=0)


def tile_count(tiles, columns):
    count = min(tiles, max(1, TILE // columns // LANES))
    while tiles % count:
        count -= 1
    return count


def early_kernel(capacity, chunks, parts, *refs):
    sources, (units, labels_out, running) = refs[:-3], refs[-3:]
    labels = unpack(sources, parts, units, capacity, chunks)
    labels_out[...] = labels
    columns = as_columns(labels)
    rows = units.shape[0]
    found = [jnp.full((EXTRA, LANES), -1.0, jnp.float32) for _ in range(rows // LANES)]
    span = tile_count(rows // LANES, rows) * LANES
    for start in range(0, rows, span):
        tiles = pieces_of(columns[start:start + span], labels[:1], units[pl.ds(start, span), :], units[...], start)
        found = [jnp.maximum(old, fold(tile)) for old, tile in zip(found, tiles)]
    for index, value in enumerate(found):
        running[:, pl.ds(index * LANES, LANES)] = value


def late_kernel(capacity, chunks, parts, keys, early_units, early_labels, running, *refs):
    sources, (target, units) = refs[:-2], refs[-2:]
    me = lax.axis_index("owner")
    lane = lax.broadcasted_iota(jnp.int32, (1, LANES), 1)
    labels = unpack(sources, parts, units, capacity, chunks)
    columns = as_columns(labels)
    old = early_units.shape[0] // LANES
    new = units.shape[0] // LANES
    found = [running[:, pl.ds(index * LANES, LANES)] for index in range(old)]
    found += [jnp.full((EXTRA, LANES), -1.0, jnp.float32) for _ in range(new)]
    count = tile_count(new, (old + new) * LANES)
    for first in range(0, new, count):
        rows = pl.ds(first * LANES, count * LANES)
        here = columns[first * LANES:(first + count) * LANES]
        tiles = pieces_of(here, early_labels[:1, :], units[rows, :], early_units[...], None)
        across = functools.reduce(jnp.maximum, tiles)
        for index in range(count):
            turned = fold(jnp.transpose(across[index * LANES:(index + 1) * LANES]))
            found[old + first + index] = jnp.maximum(found[old + first + index], turned)
        tiles += pieces_of(here, labels[:1], units[rows, :], units[...], first * LANES)
        found = [jnp.maximum(value, fold(tile)) for value, tile in zip(found, tiles)]
    for index, value in enumerate(found):
        best = jnp.max(value, axis=0, keepdims=True)
        for part in range(2):
            kept = jnp.where(lane // capacity == part, best, 0.0)
            target[jnp.bitwise_xor(me, keys[index * 2 + part])] = kept + pltpu.roll(kept, capacity, 1)


def vmem(count):
    return [pl.BlockSpec(memory_space=pltpu.VMEM)] * count


def early_best(sources, parts, capacity, width):
    rows = len(sources) * capacity
    return pl.pallas_call(
        functools.partial(early_kernel, capacity, width // LANES, parts),
        out_shape=[
            jax.ShapeDtypeStruct((rows, width), jnp.bfloat16),
            jax.ShapeDtypeStruct((EXTRA, rows), jnp.float32),
            jax.ShapeDtypeStruct((EXTRA, rows), jnp.float32),
        ],
        in_specs=vmem(len(sources)),
        out_specs=vmem(3),
        compiler_params=pltpu.CompilerParams(vmem_limit_bytes=rows * (width * 2 + 4096) + (8 << 20)),
        name="early",
    )(*sources)


def late_best(early, keys, sources, parts, capacity, width):
    rows = len(sources) * capacity
    return pl.pallas_call(
        functools.partial(late_kernel, capacity, width // LANES, parts, keys),
        out_shape=jax.ShapeDtypeStruct((len(keys), 1, LANES), jnp.float32),
        in_specs=vmem(3 + len(sources)),
        out_specs=pl.BlockSpec(memory_space=pltpu.VMEM),
        scratch_shapes=[pltpu.VMEM((rows, width), jnp.bfloat16)],
        compiler_params=pltpu.CompilerParams(vmem_limit_bytes=len(keys) * capacity * 4096 + (8 << 20)),
        name="late",
    )(*early, *sources)


def finish_kernel(capacity, source, target):
    lane = lax.broadcasted_iota(jnp.int32, (1, LANES), 1)
    for row in range(target.shape[0]):
        target[pl.ds(row, 1), :] = jnp.where(lane < capacity, source[2 * row], source[2 * row + 1])


def finish(returned, capacity):
    return pl.pallas_call(
        functools.partial(finish_kernel, capacity),
        out_shape=jax.ShapeDtypeStruct((returned.shape[0] // 2, LANES), jnp.float32),
        in_specs=vmem(1),
        out_specs=pl.BlockSpec(memory_space=pltpu.VMEM),
        compiler_params=pltpu.CompilerParams(vmem_limit_bytes=2 << 20),
        name="finish",
    )(returned)


def plan(owners):
    span = owners // 8
    keys = [top * span + low for top in ORDER for low in range(span)]
    chips = [key // 2 for key in keys[:-span] if key % 2 == 0]
    waiting = span // 2
    return chips[:-waiting] + list(range(1, waiting)), chips[-waiting:], keys[-span:]


def shift(value, key, owners):
    return lax.ppermute(value, "owner", [(i, i ^ key) for i in range(owners)])


def on_device(embeddings, cluster, lengths):
    owners = lax.axis_size("owner")
    rows_here, width = embeddings.shape
    capacity = rows_here // owners
    cluster = cluster.reshape(rows_here // LANES, LANES)
    chips, waiting, late = plan(owners)
    items = [(2 * chip, 2 * chip + 1) for chip in chips + waiting] + [(key,) for key in late] + [(0, 1)]
    cut = CUT * max(1, owners // 16)
    sent = {}
    for group in (items[:cut], items[cut:]):
        sent.update(zip(group, pack(group, lengths, cluster, embeddings, capacity)))
    mine = {}
    for item in items[:-1]:
        mine[item] = shift(sent[item], item[0], owners)
    mine[(0, 1)] = sent[(0, 1)]
    pairs = [(0, 1)] + [(2 * chip, 2 * chip + 1) for chip in chips]
    slow = [(2 * chip, 2 * chip + 1) for chip in waiting]
    other = {}
    for item in pairs + slow:
        other[item] = shift(mine[item], 1, owners)
    keys = [key for item in pairs for key in item]
    sources = [source for item in pairs for source in (mine[item], other[item])]
    early = early_best(sources, [0, 1] * len(pairs), capacity, width)
    keys += [key for item in slow for key in item] + late
    sources = [source for item in slow for source in (mine[item], other[item])]
    sources += [mine[(key,)] for key in late]
    found = late_best(early, keys, sources, [0, 1] * len(slow) + [0] * len(late), capacity, width)
    returned = lax.all_to_all(found, "owner", split_axis=0, concat_axis=0, tiled=True)
    return finish(returned, capacity).reshape(rows_here)


def solution(mesh):
    return jax.shard_map(
        on_device,
        mesh=mesh,
        in_specs=(P(("parts", "owner"), None), P(("parts", "owner")), P(("parts", "owner"), None)),
        out_specs=P(("parts", "owner")),
        check_vma=False,
    )
```

```python
import functools
import math

import jax
import jax.numpy as jnp
from jax import lax
from jax.experimental import pallas as pl
from jax.experimental.pallas import tpu as pltpu
from jax.sharding import PartitionSpec as P


LANES = 128
EXTRA = 8
TILE = 1 << 20
ORDER = (6, 2, 5, 3, 1, 4, 7)
CUT = 1
DIRECT = 2


def normalize(block, width):
    values = block.astype(jnp.float32)
    mean = jnp.mean(values * values, axis=-1, keepdims=True)
    factor = lax.rsqrt(mean + 1e-06) / math.sqrt(width)
    return (values * factor).astype(jnp.bfloat16)


def label_row(block, capacity, lengths_ref, cluster_ref):
    row = cluster_ref[pl.ds(block // 2, 1), :]
    lane = lax.broadcasted_iota(jnp.int32, (1, LANES), 1)
    kept = jnp.where(lane // capacity == block % 2, row, 0)
    spread = kept + pltpu.roll(kept, capacity, 1)
    owner = lax.broadcasted_iota(jnp.int32, lengths_ref.shape, 1)
    limit = jnp.sum(jnp.where(owner == block, lengths_ref[...], 0), axis=1, keepdims=True)
    return jnp.where(lane % capacity < limit, spread, -1)


def pack_kernel(items, capacity, width, embeddings, lengths, cluster, *refs):
    count = len(items)
    targets, (blocks, lengths_here, cluster_here, arrived) = refs[:count], refs[count:]
    chunks = width // LANES
    me = lax.axis_index("owner")
    keys = [key for item in items for key in item]
    copies = []
    for index, key in enumerate(keys):
        first = pl.multiple_of(jnp.bitwise_xor(me, key) * capacity, capacity)
        copies.append(pltpu.make_async_copy(embeddings.at[pl.ds(first, capacity), :], blocks.at[index], arrived.at[index]))
    small = [
        pltpu.make_async_copy(lengths, lengths_here, arrived.at[len(keys)]),
        pltpu.make_async_copy(cluster, cluster_here, arrived.at[len(keys) + 1]),
    ]
    for copy in copies[:1] + small + copies[1:]:
        copy.start()
    for copy in small + copies:
        copy.wait()
    lane = lax.broadcasted_iota(jnp.int32, (1, LANES), 1)
    for item, target in zip(items, targets):
        rows = [label_row(jnp.bitwise_xor(me, key), capacity, lengths_here, cluster_here) for key in item]
        labels = rows[0] if len(rows) == 1 else jnp.where(lane < capacity, rows[0], rows[1])
        labels = jnp.broadcast_to(labels.astype(jnp.float32), (EXTRA, LANES)).astype(jnp.bfloat16)
        target[pl.ds(len(item) * chunks * capacity, EXTRA), :] = labels
    index = 0
    for item, target in zip(items, targets):
        for part in range(len(item)):
            units = normalize(blocks[index], width)
            for chunk in range(chunks):
                first = (part * chunks + chunk) * capacity
                target[pl.ds(first, capacity), :] = units[:, chunk * LANES:(chunk + 1) * LANES]
            index += 1


def pack(items, lengths, cluster, embeddings, capacity):
    width = embeddings.shape[1]
    chunks = width // LANES
    keys = sum(len(item) for item in items)
    inputs = [pltpu.with_memory_space_constraint(a, pltpu.HBM) for a in (embeddings, lengths, cluster)]
    return pl.pallas_call(
        functools.partial(pack_kernel, items, capacity, width),
        out_shape=[
            jax.ShapeDtypeStruct((len(item) * chunks * capacity + EXTRA, LANES), jnp.bfloat16) for item in items
        ],
        in_specs=[pl.BlockSpec(memory_space=pltpu.HBM)] * 3,
        out_specs=vmem(len(items)),
        scratch_shapes=[
            pltpu.VMEM((keys, capacity, width), jnp.bfloat16),
            pltpu.VMEM(lengths.shape, jnp.int32),
            pltpu.VMEM(cluster.shape, jnp.int32),
            pltpu.SemaphoreType.DMA((keys + 2,)),
        ],
        compiler_params=pltpu.CompilerParams(vmem_limit_bytes=keys * capacity * width * 6 + (4 << 20)),
        name="pack",
    )(*inputs)


def unpack(sources, parts, units, capacity, chunks):
    lane = lax.broadcasted_iota(jnp.int32, (1, LANES), 1)
    rows = []
    for index, (source, part) in enumerate(zip(sources, parts)):
        for chunk in range(chunks):
            value = source[pl.ds((part * chunks + chunk) * capacity, capacity), :]
            units[pl.ds(index * capacity, capacity), pl.ds(chunk * LANES, LANES)] = value
        rows.append(source[pl.ds(source.shape[0] - EXTRA, EXTRA), :].astype(jnp.float32))
    merged = [jnp.where(lane < capacity, rows[index], rows[index + 1]) for index in range(0, len(rows), 2)]
    return jnp.concatenate(merged, axis=1) if len(merged) > 1 else merged[0]


def as_columns(labels):
    return jnp.transpose(labels)[:, :1]


def similarity(left, right):
    return lax.dot_general(left, right, (((1,), (1,)), ((), ())), preferred_element_type=jnp.float32)


def pieces_of(columns, row_labels, left, right, first):
    similar = similarity(left, right)
    alive = jnp.where(row_labels < 0, -2.0, row_labels)
    masked = jnp.where(columns == alive, similar, -1.0)
    tiles = [masked[:, start:start + LANES] for start in range(0, masked.shape[1], LANES)]
    if first is not None:
        row = lax.broadcasted_iota(jnp.int32, (left.shape[0], LANES), 0)
        lane = lax.broadcasted_iota(jnp.int32, (left.shape[0], LANES), 1)
        for start in range(0, left.shape[0], LANES):
            own = (first + start) // LANES
            tiles[own] = jnp.where(row != lane + start, tiles[own], -1.0)
    return tiles


def fold(tile):
    return jnp.max(tile.reshape(tile.shape[0] // EXTRA, EXTRA, LANES), axis=0)


def tile_count(tiles, columns):
    count = min(tiles, max(1, TILE // columns // LANES))
    while tiles % count:
        count -= 1
    return count


def early_kernel(capacity, chunks, parts, *refs):
    sources, (units, labels_out, running) = refs[:-3], refs[-3:]
    labels = unpack(sources, parts, units, capacity, chunks)
    labels_out[...] = labels
    columns = as_columns(labels)
    rows = units.shape[0]
    found = [jnp.full((EXTRA, LANES), -1.0, jnp.float32) for _ in range(rows // LANES)]
    span = tile_count(rows // LANES, rows) * LANES
    for start in range(0, rows, span):
        tiles = pieces_of(columns[start:start + span], labels[:1], units[pl.ds(start, span), :], units[...], start)
        found = [jnp.maximum(old, fold(tile)) for old, tile in zip(found, tiles)]
    for index, value in enumerate(found):
        running[:, pl.ds(index * LANES, LANES)] = value


def late_kernel(capacity, chunks, keys, early_units, early_labels, running, *refs):
    sources, (target, units) = refs[:-2], refs[-2:]
    me = lax.axis_index("owner")
    lane = lax.broadcasted_iota(jnp.int32, (1, LANES), 1)
    labels = unpack(sources, [0] * len(sources), units, capacity, chunks)
    columns = as_columns(labels)
    old = early_units.shape[0] // LANES
    new = units.shape[0] // LANES
    found = [running[:, pl.ds(index * LANES, LANES)] for index in range(old)]
    found += [jnp.full((EXTRA, LANES), -1.0, jnp.float32) for _ in range(new)]
    count = tile_count(new, (old + new) * LANES)
    for first in range(0, new, count):
        rows = pl.ds(first * LANES, count * LANES)
        here = columns[first * LANES:(first + count) * LANES]
        tiles = pieces_of(here, early_labels[:1, :], units[rows, :], early_units[...], None)
        across = functools.reduce(jnp.maximum, tiles)
        for index in range(count):
            turned = fold(jnp.transpose(across[index * LANES:(index + 1) * LANES]))
            found[old + first + index] = jnp.maximum(found[old + first + index], turned)
        tiles += pieces_of(here, labels[:1], units[rows, :], units[...], first * LANES)
        found = [jnp.maximum(value, fold(tile)) for value, tile in zip(found, tiles)]
    for index, value in enumerate(found):
        best = jnp.max(value, axis=0, keepdims=True)
        for part in range(2):
            kept = jnp.where(lane // capacity == part, best, 0.0)
            target[jnp.bitwise_xor(me, keys[index * 2 + part])] = kept + pltpu.roll(kept, capacity, 1)


def vmem(count):
    return [pl.BlockSpec(memory_space=pltpu.VMEM)] * count


def early_best(sources, parts, capacity, width):
    rows = len(sources) * capacity
    return pl.pallas_call(
        functools.partial(early_kernel, capacity, width // LANES, parts),
        out_shape=[
            jax.ShapeDtypeStruct((rows, width), jnp.bfloat16),
            jax.ShapeDtypeStruct((EXTRA, rows), jnp.float32),
            jax.ShapeDtypeStruct((EXTRA, rows), jnp.float32),
        ],
        in_specs=vmem(len(sources)),
        out_specs=vmem(3),
        compiler_params=pltpu.CompilerParams(vmem_limit_bytes=rows * (width * 2 + 4096) + (8 << 20)),
        name="early",
    )(*sources)


def late_best(early, keys, sources, capacity, width):
    rows = len(sources) * capacity
    return pl.pallas_call(
        functools.partial(late_kernel, capacity, width // LANES, keys),
        out_shape=jax.ShapeDtypeStruct((len(keys), 1, LANES), jnp.float32),
        in_specs=vmem(3 + len(sources)),
        out_specs=pl.BlockSpec(memory_space=pltpu.VMEM),
        scratch_shapes=[pltpu.VMEM((rows, width), jnp.bfloat16)],
        compiler_params=pltpu.CompilerParams(vmem_limit_bytes=len(keys) * capacity * 4096 + (8 << 20)),
        name="late",
    )(*early, *sources)


def finish_kernel(capacity, source, target):
    lane = lax.broadcasted_iota(jnp.int32, (1, LANES), 1)
    for row in range(target.shape[0]):
        target[pl.ds(row, 1), :] = jnp.where(lane < capacity, source[2 * row], source[2 * row + 1])


def finish(returned, capacity):
    return pl.pallas_call(
        functools.partial(finish_kernel, capacity),
        out_shape=jax.ShapeDtypeStruct((returned.shape[0] // 2, LANES), jnp.float32),
        in_specs=vmem(1),
        out_specs=pl.BlockSpec(memory_space=pltpu.VMEM),
        compiler_params=pltpu.CompilerParams(vmem_limit_bytes=2 << 20),
        name="finish",
    )(returned)


def plan(owners):
    span = owners // 8
    keys = [top * span + low for top in ORDER for low in range(span)]
    chips = [key // 2 for key in keys[:-DIRECT * span] if key % 2 == 0]
    return chips + list(range(1, span // 2)), keys[-DIRECT * span:]


def shift(value, key, owners):
    return lax.ppermute(value, "owner", [(i, i ^ key) for i in range(owners)])


def on_device(embeddings, cluster, lengths):
    owners = lax.axis_size("owner")
    rows_here, width = embeddings.shape
    capacity = rows_here // owners
    cluster = cluster.reshape(rows_here // LANES, LANES)
    chips, late = plan(owners)
    items = [(2 * chip, 2 * chip + 1) for chip in chips] + [(key,) for key in late] + [(0, 1)]
    cut = CUT * max(1, owners // 16)
    sent = {}
    for group in (items[:cut], items[cut:]):
        sent.update(zip(group, pack(group, lengths, cluster, embeddings, capacity)))
    mine = {}
    for item in items[:-1]:
        mine[item] = shift(sent[item], item[0], owners)
    mine[(0, 1)] = sent[(0, 1)]
    pairs = [(0, 1)] + [(2 * chip, 2 * chip + 1) for chip in chips]
    other = {}
    for item in pairs:
        other[item] = shift(mine[item], 1, owners)
    keys = [key for item in pairs for key in item]
    sources = [source for item in pairs for source in (mine[item], other[item])]
    early = early_best(sources, [0, 1] * len(pairs), capacity, width)
    found = late_best(early, keys + late, [mine[(key,)] for key in late], capacity, width)
    returned = lax.all_to_all(found, "owner", split_axis=0, concat_axis=0, tiled=True)
    return finish(returned, capacity).reshape(rows_here)


def solution(mesh):
    return jax.shard_map(
        on_device,
        mesh=mesh,
        in_specs=(P(("parts", "owner"), None), P(("parts", "owner")), P(("parts", "owner"), None)),
        out_specs=P(("parts", "owner")),
        check_vma=False,
    )
```
